1024 devices in a mesh: dp: 32 (over z, core), ctx: 16 (over y_lo, x), chan: 2 (over y_hi).
Axes of the slice: x: 4, y: 8 (y_hi: 2, y_lo: 4; y = y_hi * 4 + y_lo), z: 16, core: 2. Of those that a mesh axis runs over, the one named last changes fastest.
Arguments:
- layer_input: bfloat16 [4096, 16384], P(('dp', 'chan'), 'ctx'), may hold values from -6 to 6
- grad_output: bfloat16 [4096, 16384], P(('dp', 'chan'), 'ctx'), may hold values from -6 to 6
- filter_taps: float32 [64, 64, 16384], P(('dp', 'chan'), 'ctx'), may hold values from -2 to 2
Outputs:
- grad_input: bfloat16 [4096, 16384], P(('dp', 'chan'), 'ctx')
- grad_filter: float32 [64, 64, 16384], P(('dp', 'chan'), 'ctx')
The draws below stay inside these ranges and needn't reach their ends.
All inputs are finite; a program needn't handle non-finite values.
Results may differ from the reference program's by a relative error of at most 0.001.
Values may be sent and summed in bfloat16 or wider, within the bound.
A program may use at most 32 MiB of HBM per device.

```python
import math
import jax
import jax.numpy as jnp
from jax import lax

CHANNELS = 4096
LENGTH = 16384
CHAN_DEV = 64


def draw_filter_taps(key, part):
    key_rate, key_pick, key_noise, key_lag = jax.random.split(key, 4)
    group_count = CHANNELS // CHAN_DEV
    kernel_coefficient_dims = (group_count, CHAN_DEV, LENGTH)
    slow_low = math.log(0.25 / LENGTH)
    slow_high = math.log(2.0 / LENGTH)
    fast_high = math.log(1.0 / 20.0)
    pick = jax.random.uniform(key_pick, (group_count, CHAN_DEV, 1), jnp.float32)
    unit = jax.random.uniform(key_rate, (group_count, CHAN_DEV, 1), jnp.float32)
    slow_rate = jnp.exp(slow_low + unit * (slow_high - slow_low))
    fast_rate = jnp.exp(slow_high + unit * (fast_high - slow_high))
    slow_share = 0.5
    gaussian_perturbation = jnp.clip(jax.random.normal(key_noise, kernel_coefficient_dims, jnp.float32), -4.0, 4.0)
    fading_speed = jnp.where(pick < slow_share, slow_rate, fast_rate)
    lag_position = lax.broadcasted_iota(jnp.int32, kernel_coefficient_dims, 2)
    lag_shifts = jax.random.randint(key_lag, (3, group_count, CHAN_DEV, 1), 1, LENGTH)
    spike_height = jnp.ones(kernel_coefficient_dims, jnp.float32)
    for batch_members in range(3):
        spike_height = spike_height * jnp.where(lag_position >= lag_shifts[batch_members], 0.6, 1.0)
    fading_multiplier = jnp.exp(-fading_speed * lag_position.astype(jnp.float32))
    kernel_coefficients = jnp.sqrt(2.0 * fading_speed) * fading_multiplier * gaussian_perturbation * spike_height
    return kernel_coefficients.astype(jnp.float32)


def block_levels(own_key, shape, shards, least, top_value):
    factor_of = 1.0
    for axis_at, parts in shards:
        draws = jax.random.uniform(jax.random.fold_in(jax.random.fold_in(own_key, 6), axis_at), (parts,), jnp.float32, least / len(shards), top_value / len(shards))
        factor_of = factor_of * jnp.repeat(jnp.exp(draws), shape[axis_at] // parts).reshape((-1,) + (1,) * (len(shape) - 1 - axis_at))
    return factor_of


def noise(stream_key, dims, deviation, reach, cuts=(), kind=jnp.bfloat16):
    entries = deviation * jax.random.normal(stream_key, dims, jnp.float32)
    if cuts:
        entries = entries * block_levels(stream_key, dims, cuts, -0.22, 0.18)
    return jnp.clip(entries, -reach, reach).astype(kind)


def setup_inputs(seed: int = 0) -> dict:
    streams_of = jax.random.split(jax.random.key(seed), 4)
    layer_input = noise(streams_of[0], (CHANNELS, LENGTH), 1.0, 6.0, ((0, 64), (1, 16)))
    grad_output = noise(streams_of[1], (CHANNELS, LENGTH), 1.0, 6.0, ((0, 64), (1, 16)))
    filter_taps = draw_filter_taps(jax.random.fold_in(streams_of[3], 71), 0)
    return dict(layer_input=layer_input, grad_output=grad_output, filter_taps=filter_taps)


def reference(layer_input, grad_output, filter_taps):
    size_fft = 2 * LENGTH
    block = min(256, CHANNELS)
    block_count = CHANNELS // block
    taps = filter_taps.reshape(block_count, block, LENGTH)
    inputs = layer_input.reshape(block_count, block, LENGTH)
    grads = grad_output.reshape(block_count, block, LENGTH)

    def one_block(pieces):
        input_rows, grad_rows, filter_rows = pieces
        input_spec = jnp.fft.rfft(input_rows.astype(jnp.float32), n=size_fft, axis=1)
        grad_spec = jnp.fft.rfft(grad_rows.astype(jnp.float32), n=size_fft, axis=1)
        filter_spec = jnp.fft.rfft(filter_rows, n=size_fft, axis=1)
        back = jnp.fft.irfft(jnp.conj(filter_spec) * grad_spec, n=size_fft, axis=1)[:, :LENGTH]
        corr = jnp.fft.irfft(grad_spec * jnp.conj(input_spec), n=size_fft, axis=1)[:, :LENGTH]
        return (back.astype(jnp.bfloat16), (corr / math.sqrt(LENGTH)).astype(jnp.float32))
    grad_input, grad_filter = lax.map(one_block, (inputs, grads, taps))
    grad_input = grad_input.reshape(CHANNELS, LENGTH)
    grad_filter = grad_filter.reshape(filter_taps.shape)
    return (grad_input, grad_filter)
```

```python
import math

import jax
import jax.numpy as jnp
import numpy as np
from jax import lax
from jax.experimental import pallas as pl
from jax.experimental.pallas import tpu as pltpu
from jax.sharding import PartitionSpec as P

import ml_dtypes

BF = jnp.bfloat16
F32 = jnp.float32
SIDE = 128
PEERS = 16
PENCIL = 4
MESH = pl.DeviceIdType.MESH


def split_table(values):
    high = values.astype(ml_dtypes.bfloat16)
    low = (values - high.astype(np.float64)).astype(ml_dtypes.bfloat16)
    return high, low


def make_tables():
    total = SIDE * SIDE
    index = np.arange(SIDE, dtype=np.int64)
    first = ((4 * index[:, None] + 1) * index[None, :]) % (4 * SIDE) * (2.0 * np.pi / (4 * SIDE))
    first_high, first_low = split_table(np.concatenate([np.cos(first), -np.sin(first)], axis=0))
    forward_first = np.concatenate([first_high, first_low, first_high], axis=1)
    turn = ((4 * index[:, None] + 1) * index[None, :]) % (4 * total) * (2.0 * np.pi / (4 * total))
    turns = np.stack([np.cos(turn), np.sin(turn)]).astype(np.float32)
    second = (index[:, None] * index[None, :]) % SIDE * (2.0 * np.pi / SIDE)
    cos_two, sin_two = np.cos(second), np.sin(second)
    high, low = split_table(np.block([[cos_two, -sin_two], [sin_two, cos_two]]))
    forward_second = np.concatenate([high, high, low], axis=0)
    high, low = split_table(np.block([[cos_two, sin_two], [-sin_two, cos_two]]))
    inverse_second = np.concatenate([high, high, low], axis=0)
    high, low = split_table(np.concatenate([np.cos(first).T, -np.sin(first).T], axis=1) / total)
    inverse_first = np.concatenate([high, high, low], axis=1)
    return forward_first, forward_second, inverse_second, inverse_first, turns


def halves(value):
    high = value.astype(BF)
    return high, (value - high.astype(F32)).astype(BF)


def second_stage(first, turns_v, second_v):
    real, imag = first[:SIDE], first[SIDE:]
    cos_turn, sin_turn = turns_v[0], turns_v[1]
    real_high, real_low = halves(real * cos_turn + imag * sin_turn)
    imag_high, imag_low = halves(imag * cos_turn - real * sin_turn)
    stacked = jnp.concatenate([real_high, imag_high, real_low, imag_low, real_high, imag_high], axis=1)
    return jnp.dot(stacked, second_v[...], preferred_element_type=F32)


def inverse(real, imag, turns_v, inverse_second_v, inverse_first_v):
    real_high, real_low = halves(real)
    imag_high, imag_low = halves(imag)
    stacked = jnp.concatenate([real_high, imag_high, real_low, imag_low, real_high, imag_high], axis=1)
    mixed = jnp.dot(stacked, inverse_second_v[...], preferred_element_type=F32)
    real, imag = mixed[:, :SIDE], mixed[:, SIDE:]
    cos_turn, sin_turn = turns_v[0], turns_v[1]
    real_high, real_low = halves(real * cos_turn - imag * sin_turn)
    imag_high, imag_low = halves(imag * cos_turn + real * sin_turn)
    stacked = jnp.concatenate([real_high, imag_high, real_low, imag_low, real_high, imag_high], axis=0)
    return jnp.dot(inverse_first_v[...], stacked, preferred_element_type=F32)


def kernel(
    grad_hbm,
    input_hbm,
    taps_hbm,
    first_hbm,
    second_hbm,
    inverse_second_hbm,
    inverse_first_hbm,
    turns_hbm,
    grad_input_v,
    grad_taps_v,
    grad_v,
    input_v,
    taps_v,
    first_v,
    second_v,
    inverse_second_v,
    inverse_first_v,
    turns_v,
    turned_v,
    send_grad,
    send_input,
    send_back,
    got_grad,
    got_input,
    got_back,
    taps_spec,
    grad_spec,
    local_sem,
    send_sem,
    recv_sem,
):
    me = lax.axis_index("ctx")

    def load(source, target, slot):
        copy = pltpu.make_async_copy(source, target, local_sem.at[slot])
        copy.start()
        return copy

    grad_load = load(grad_hbm, grad_v, 0)
    input_load = load(input_hbm, input_v, 1)
    later_loads = [
        load(source, target, slot)
        for slot, (source, target) in enumerate(
            (
                (taps_hbm, taps_v),
                (first_hbm, first_v),
                (turns_hbm, turns_v),
                (second_hbm, second_v),
                (inverse_second_hbm, inverse_second_v),
                (inverse_first_hbm, inverse_first_v),
            ),
            2,
        )
    ]

    barrier = pltpu.get_barrier_semaphore()

    @pl.loop(1, PEERS)
    def _(step):
        pl.semaphore_signal(
            barrier, inc=1, device_id={"ctx": lax.rem(me + step, PEERS)}, device_id_type=MESH
        )

    def turn_rows(source, target):
        for group in range(8):
            turned_v[group] = source[group].astype(F32).reshape(64, SIDE)
            for row in range(8):
                picked = turned_v[group, pl.ds(row, 8, stride=8), :]
                target[2 * group + row // 4, row % 4] = picked.astype(BF)

    def exchange(source, target, slot):
        @pl.loop(1, PEERS)
        def _(step):
            peer = lax.rem(me + step, PEERS)
            pltpu.make_async_remote_copy(
                src_ref=source.at[peer],
                dst_ref=target.at[me],
                send_sem=send_sem.at[slot],
                recv_sem=recv_sem.at[slot],
                device_id={"ctx": peer},
                device_id_type=MESH,
            ).start()

        target[me] = source[me]

    def all_of(source, target, slot):
        return pltpu.make_async_remote_copy(
            src_ref=source.at[pl.ds(0, PEERS - 1)],
            dst_ref=target.at[pl.ds(0, PEERS - 1)],
            send_sem=send_sem.at[slot],
            recv_sem=recv_sem.at[slot],
            device_id={"ctx": lax.rem(me + 1, PEERS)},
            device_id_type=MESH,
        )

    grad_load.wait()
    turn_rows(grad_v, send_grad)
    pl.semaphore_wait(barrier, PEERS - 1)
    exchange(send_grad, got_grad, 0)
    input_load.wait()
    turn_rows(input_v, send_input)
    exchange(send_input, got_input, 1)

    for copy in later_loads:
        copy.wait()

    for channel in range(PENCIL):
        high, low = halves(taps_v[pl.ds(channel, SIDE, stride=PENCIL), :])
        first = jnp.dot(
            first_v[...], jnp.concatenate([high, high, low], axis=0), preferred_element_type=F32
        )
        taps_spec[channel] = second_stage(first, turns_v, second_v)

    def forward(source, channel):
        rows = source[:, channel].reshape(SIDE, SIDE)
        first = jnp.dot(
            first_v[:, : 2 * SIDE], jnp.concatenate([rows, rows], axis=0), preferred_element_type=F32
        )
        return second_stage(first, turns_v, second_v)

    all_of(send_grad, got_grad, 0).wait_recv()
    for channel in range(PENCIL):
        spectrum = forward(got_grad, channel)
        grad_spec[channel] = spectrum
        grad_real, grad_imag = spectrum[:, :SIDE], spectrum[:, SIDE:]
        taps_real, taps_imag = taps_spec[channel, :, :SIDE], taps_spec[channel, :, SIDE:]
        back = inverse(
            taps_real * grad_real + taps_imag * grad_imag,
            taps_real * grad_imag - taps_imag * grad_real,
            turns_v,
            inverse_second_v,
            inverse_first_v,
        )
        send_back[:, channel] = back.astype(BF).reshape(PEERS, 8, SIDE)
    exchange(send_back, got_back, 2)

    all_of(send_input, got_input, 1).wait_recv()
    for channel in range(PENCIL):
        spectrum = forward(got_input, channel)
        input_real, input_imag = spectrum[:, :SIDE], spectrum[:, SIDE:]
        grad_real, grad_imag = grad_spec[channel, :, :SIDE], grad_spec[channel, :, SIDE:]
        lags = inverse(
            grad_real * input_real + grad_imag * input_imag,
            grad_imag * input_real - grad_real * input_imag,
            turns_v,
            inverse_second_v,
            inverse_first_v,
        )
        grad_taps_v[pl.ds(channel, SIDE, stride=PENCIL), :] = lags * (1.0 / SIDE)

    all_of(send_back, got_back, 2).wait_recv()
    for group in range(8):
        for row in range(8):
            turned_v[group, pl.ds(8 * row, 8), :] = got_back[2 * group + row // 4, row % 4].astype(F32)
        for block in range(8):
            grad_input_v[group, block] = turned_v[group, pl.ds(block, 8, stride=8), :].astype(BF)
    for slot, (source, target) in enumerate(
        ((send_grad, got_grad), (send_input, got_input), (send_back, got_back))
    ):
        all_of(source, target, slot).wait_send()


def shards(layer_input, grad_output, filter_taps):
    rows, width = layer_input.shape
    blocks = width // SIDE
    tiles = (rows // 8, 8, blocks, SIDE)
    tables = make_tables()
    taps = filter_taps.reshape(PENCIL, SIDE, SIDE).transpose(1, 0, 2).reshape(PENCIL * SIDE, SIDE)
    tile_shape = (rows // 8, blocks, 8, SIDE)
    block_shape = (PEERS, PENCIL, blocks, SIDE)
    operands = (
        grad_output.reshape(tiles).transpose(0, 2, 1, 3),
        layer_input.reshape(tiles).transpose(0, 2, 1, 3),
        taps,
        *[jnp.asarray(table) for table in tables],
    )
    grad_input, grad_taps = pl.pallas_call(
        kernel,
        name="conv_backward",
        out_shape=(
            pltpu.VMEM(tile_shape, BF),
            pltpu.VMEM((PENCIL * SIDE, SIDE), F32),
        ),
        in_specs=[pl.BlockSpec(memory_space=pltpu.HBM)] * 8,
        out_specs=[pl.BlockSpec(memory_space=pltpu.VMEM)] * 2,
        scratch_shapes=[
            pltpu.VMEM(tile_shape, BF),
            pltpu.VMEM(tile_shape, BF),
            pltpu.VMEM((PENCIL * SIDE, SIDE), F32),
            *[pltpu.VMEM(table.shape, F32 if table.dtype == np.float32 else BF) for table in tables],
            pltpu.VMEM((8, 64, SIDE), F32),
            *[pltpu.VMEM(block_shape, BF)] * 6,
            pltpu.VMEM((PENCIL, SIDE, 2 * SIDE), F32),
            pltpu.VMEM((PENCIL, SIDE, 2 * SIDE), F32),
            pltpu.SemaphoreType.DMA((8,)),
            pltpu.SemaphoreType.DMA((3,)),
            pltpu.SemaphoreType.DMA((3,)),
        ],
        compiler_params=pltpu.CompilerParams(
            collective_id=0, has_side_effects=True, vmem_limit_bytes=48 * 1024 * 1024
        ),
    )(*[pltpu.with_memory_space_constraint(operand, pltpu.HBM) for operand in operands])
    grad_input = grad_input.transpose(0, 2, 1, 3).reshape(rows, width)
    grad_taps = grad_taps.reshape(SIDE, PENCIL, SIDE).transpose(1, 0, 2)
    return grad_input, grad_taps.reshape(1, PENCIL, SIDE * SIDE)


def solution(mesh):
    in_specs = (P(("dp", "chan"), "ctx"), P(("dp", "chan"), "ctx"), P(("dp", "chan"), "ctx", None))
    out_specs = (P(("dp", "chan"), "ctx"), P(("dp", "chan"), "ctx", None))
    return jax.shard_map(shards, mesh=mesh, in_specs=in_specs, out_specs=out_specs, check_vma=False)
```

```python
import math

import jax
import jax.numpy as jnp
import numpy as np
from jax import lax
from jax.experimental import pallas as pl
from jax.experimental.pallas import tpu as pltpu
from jax.sharding import PartitionSpec as P

import ml_dtypes

BF = jnp.bfloat16
F32 = jnp.float32
SIDE = 128
PEERS = 16
PENCIL = 4
BATCH = 4
MESH = pl.DeviceIdType.MESH
FAR_FIRST = (
    (3, 2), (3, 1), (3, 3), (2, 2), (2, 1), (2, 3), (3, 0), (1, 2),
    (2, 0), (1, 1), (1, 3), (0, 2), (1, 0), (0, 1), (0, 3),
)


def split_table(values):
    high = values.astype(ml_dtypes.bfloat16)
    low = (values - high.astype(np.float64)).astype(ml_dtypes.bfloat16)
    return high, low


def make_tables():
    total = SIDE * SIDE
    index = np.arange(SIDE, dtype=np.int64)
    first = ((4 * index[:, None] + 1) * index[None, :]) % (4 * SIDE) * (2.0 * np.pi / (4 * SIDE))
    first_high, first_low = split_table(np.concatenate([np.cos(first), -np.sin(first)], axis=0))
    forward_first = np.concatenate([first_high, first_low, first_high], axis=1)
    turn = ((4 * index[:, None] + 1) * index[None, :]) % (4 * total) * (2.0 * np.pi / (4 * total))
    turns = np.stack([np.cos(turn), np.sin(turn)]).astype(np.float32)
    second = (index[:, None] * index[None, :]) % SIDE * (2.0 * np.pi / SIDE)
    cos_two, sin_two = np.cos(second), np.sin(second)
    high, low = split_table(np.block([[cos_two, -sin_two], [sin_two, cos_two]]))
    forward_second = np.concatenate([high, high, low], axis=0)
    high, low = split_table(np.block([[cos_two, sin_two], [-sin_two, cos_two]]))
    inverse_second = np.concatenate([high, high, low], axis=0)
    high, low = split_table(np.concatenate([np.cos(first).T, -np.sin(first).T], axis=1) / total)
    inverse_first = np.concatenate([high, high, low], axis=1)
    return forward_first, forward_second, inverse_second, inverse_first, turns


def halves(value):
    high = value.astype(BF)
    return high, (value - high.astype(F32)).astype(BF)


def stacked_rows(pairs, turned):
    blocks = []
    for real, imag in pairs:
        real_high, real_low = halves(real)
        imag_high, imag_low = halves(imag)
        parts = [real_high, imag_high, real_low, imag_low, real_high, imag_high]
        blocks.append(jnp.concatenate(parts, axis=0 if turned else 1))
    return jnp.concatenate(blocks, axis=1 if turned else 0)


def channel_parts(spectra):
    count = spectra.shape[0] // SIDE
    return [
        (spectra[at * SIDE : (at + 1) * SIDE, :SIDE], spectra[at * SIDE : (at + 1) * SIDE, SIDE:])
        for at in range(count)
    ]


def second_stage(first, turns_v, second_v):
    cos_turn, sin_turn = turns_v[0], turns_v[1]
    pairs = []
    for at in range(first.shape[1] // SIDE):
        real = first[:SIDE, at * SIDE : (at + 1) * SIDE]
        imag = first[SIDE:, at * SIDE : (at + 1) * SIDE]
        pairs.append((real * cos_turn + imag * sin_turn, imag * cos_turn - real * sin_turn))
    return jnp.dot(stacked_rows(pairs, False), second_v[...], preferred_element_type=F32)


def inverse(pairs, turns_v, inverse_second_v, inverse_first_v):
    mixed = jnp.dot(stacked_rows(pairs, False), inverse_second_v[...], preferred_element_type=F32)
    cos_turn, sin_turn = turns_v[0], turns_v[1]
    turned = [
        (real * cos_turn - imag * sin_turn, imag * cos_turn + real * sin_turn)
        for real, imag in channel_parts(mixed)
    ]
    return jnp.dot(inverse_first_v[...], stacked_rows(turned, True), preferred_element_type=F32)


def kernel(
    grad_hbm,
    input_hbm,
    taps_hbm,
    first_hbm,
    second_hbm,
    inverse_second_hbm,
    inverse_first_hbm,
    turns_hbm,
    got_back,
    grad_taps_v,
    grad_v,
    input_v,
    taps_v,
    first_v,
    second_v,
    inverse_second_v,
    inverse_first_v,
    turns_v,
    turned_v,
    send_grad,
    send_input,
    send_back,
    got_grad,
    got_input,
    taps_spec,
    grad_spec,
    local_sem,
    send_sem,
    recv_sem,
):
    me = lax.axis_index("ctx")
    row, column = me // 4, me % 4
    rows = (row, row + 1 - 2 * (row % 2), (row + 2) % 4, 3 - row)
    peers = [rows[over] * 4 + (column + along) % 4 for over, along in FAR_FIRST]

    def load(source, target, slot):
        copy = pltpu.make_async_copy(source, target, local_sem.at[slot])
        copy.start()
        return copy

    grad_load = load(grad_hbm, grad_v, 0)
    input_load = load(input_hbm, input_v, 1)
    later_loads = [
        load(source, target, slot)
        for slot, (source, target) in enumerate(
            (
                (taps_hbm, taps_v),
                (first_hbm, first_v),
                (turns_hbm, turns_v),
                (second_hbm, second_v),
                (inverse_second_hbm, inverse_second_v),
                (inverse_first_hbm, inverse_first_v),
            ),
            2,
        )
    ]

    barrier = pltpu.get_barrier_semaphore()

    for peer in peers:
        pl.semaphore_signal(barrier, inc=1, device_id={"ctx": peer}, device_id_type=MESH)

    def turn_rows(source, target):
        for group in range(8):
            turned_v[group] = source[group].astype(F32).reshape(64, SIDE)
            for row in range(8):
                picked = turned_v[group, pl.ds(row, 8, stride=8), :]
                target[2 * group + row // 4, row % 4] = picked.astype(BF)

    def exchange(source, target, slot):
        for peer in peers:
            pltpu.make_async_remote_copy(
                src_ref=source.at[peer],
                dst_ref=target.at[me],
                send_sem=send_sem.at[slot],
                recv_sem=recv_sem.at[slot],
                device_id={"ctx": peer},
                device_id_type=MESH,
            ).start()

        target[me] = source[me]

    def all_of(source, target, slot):
        return pltpu.make_async_remote_copy(
            src_ref=source.at[pl.ds(0, PEERS - 1)],
            dst_ref=target.at[pl.ds(0, PEERS - 1)],
            send_sem=send_sem.at[slot],
            recv_sem=recv_sem.at[slot],
            device_id={"ctx": lax.rem(me + 1, PEERS)},
            device_id_type=MESH,
        )

    grad_load.wait()
    turn_rows(grad_v, send_grad)
    pl.semaphore_wait(barrier, PEERS - 1)
    exchange(send_grad, got_grad, 0)
    input_load.wait()
    turn_rows(input_v, send_input)
    exchange(send_input, got_input, 1)

    for copy in later_loads:
        copy.wait()

    for start in range(0, PENCIL, BATCH):
        columns = []
        for channel in range(start, start + BATCH):
            high, low = halves(taps_v[pl.ds(channel, SIDE, stride=PENCIL), :])
            columns.append(jnp.concatenate([high, high, low], axis=0))
        first = jnp.dot(
            first_v[...], jnp.concatenate(columns, axis=1), preferred_element_type=F32
        )
        taps_spec[start * SIDE : (start + BATCH) * SIDE, :] = second_stage(first, turns_v, second_v)

    def forward(source, start):
        rows = jnp.concatenate(
            [source[:, channel].reshape(SIDE, SIDE) for channel in range(start, start + BATCH)], axis=1
        )
        first = jnp.dot(
            first_v[:, : 2 * SIDE], jnp.concatenate([rows, rows], axis=0), preferred_element_type=F32
        )
        return second_stage(first, turns_v, second_v)

    all_of(send_grad, got_grad, 0).wait_recv()
    for start in range(0, PENCIL, BATCH):
        spectra = forward(got_grad, start)
        grad_spec[start * SIDE : (start + BATCH) * SIDE, :] = spectra
        products = [
            (taps_real * real + taps_imag * imag, taps_real * imag - taps_imag * real)
            for (real, imag), (taps_real, taps_imag) in zip(
                channel_parts(spectra),
                channel_parts(taps_spec[start * SIDE : (start + BATCH) * SIDE, :]),
            )
        ]
        back = inverse(products, turns_v, inverse_second_v, inverse_first_v).astype(BF)
        for at in range(BATCH):
            block = back[:, at * SIDE : (at + 1) * SIDE]
            send_back[:, start + at] = block.reshape(PEERS, 8, SIDE)
    exchange(send_back, got_back, 2)

    all_of(send_input, got_input, 1).wait_recv()
    for start in range(0, PENCIL, BATCH):
        spectra = forward(got_input, start)
        products = [
            (grad_real * real + grad_imag * imag, grad_imag * real - grad_real * imag)
            for (real, imag), (grad_real, grad_imag) in zip(
                channel_parts(spectra),
                channel_parts(grad_spec[start * SIDE : (start + BATCH) * SIDE, :]),
            )
        ]
        lags = inverse(products, turns_v, inverse_second_v, inverse_first_v) * (1.0 / SIDE)
        for at in range(BATCH):
            grad_taps_v[pl.ds(start + at, SIDE, stride=PENCIL), :] = lags[:, at * SIDE : (at + 1) * SIDE]

    all_of(send_back, got_back, 2).wait_recv()
    for slot, (source, target) in enumerate(
        ((send_grad, got_grad), (send_input, got_input), (send_back, got_back))
    ):
        all_of(source, target, slot).wait_send()


def finish(got_back, grad_taps_v, grad_input_hbm, grad_taps_hbm, turned_v, grad_input_v, sem):
    taps_store = pltpu.make_async_copy(grad_taps_v, grad_taps_hbm, sem.at[0])
    taps_store.start()
    for group in range(8):
        for row in range(8):
            turned_v[group, pl.ds(8 * row, 8), :] = got_back[2 * group + row // 4, row % 4].astype(F32)
        for block in range(8):
            grad_input_v[group, block] = turned_v[group, pl.ds(block, 8, stride=8), :].astype(BF)
    back_store = pltpu.make_async_copy(grad_input_v, grad_input_hbm, sem.at[1])
    back_store.start()
    taps_store.wait()
    back_store.wait()


def shards(layer_input, grad_output, filter_taps):
    rows, width = layer_input.shape
    blocks = width // SIDE
    tiles = (rows // 8, 8, blocks, SIDE)
    tables = make_tables()
    taps = filter_taps.reshape(PENCIL, SIDE, SIDE).transpose(1, 0, 2).reshape(PENCIL * SIDE, SIDE)
    tile_shape = (rows // 8, blocks, 8, SIDE)
    block_shape = (PEERS, PENCIL, blocks, SIDE)
    operands = (
        grad_output.reshape(tiles).transpose(0, 2, 1, 3),
        layer_input.reshape(tiles).transpose(0, 2, 1, 3),
        taps,
        *[jnp.asarray(table) for table in tables],
    )
    back_blocks, lags = pl.pallas_call(
        kernel,
        name="conv_backward",
        out_shape=(
            pltpu.VMEM(block_shape, BF),
            pltpu.VMEM((PENCIL * SIDE, SIDE), F32),
        ),
        in_specs=[pl.BlockSpec(memory_space=pltpu.HBM)] * 8,
        out_specs=[pl.BlockSpec(memory_space=pltpu.VMEM)] * 2,
        scratch_shapes=[
            pltpu.VMEM(tile_shape, BF),
            pltpu.VMEM(tile_shape, BF),
            pltpu.VMEM((PENCIL * SIDE, SIDE), F32),
            *[pltpu.VMEM(table.shape, F32 if table.dtype == np.float32 else BF) for table in tables],
            pltpu.VMEM((8, 64, SIDE), F32),
            *[pltpu.VMEM(block_shape, BF)] * 5,
            pltpu.VMEM((PENCIL * SIDE, 2 * SIDE), F32),
            pltpu.VMEM((PENCIL * SIDE, 2 * SIDE), F32),
            pltpu.SemaphoreType.DMA((8,)),
            pltpu.SemaphoreType.DMA((3,)),
            pltpu.SemaphoreType.DMA((3,)),
        ],
        compiler_params=pltpu.CompilerParams(
            collective_id=0, has_side_effects=True, vmem_limit_bytes=48 * 1024 * 1024
        ),
    )(*[pltpu.with_memory_space_constraint(operand, pltpu.HBM) for operand in operands])
    grad_input, grad_taps = pl.pallas_call(
        finish,
        name="conv_backward_finish",
        out_shape=(
            jax.ShapeDtypeStruct(tile_shape, BF),
            jax.ShapeDtypeStruct((PENCIL * SIDE, SIDE), F32),
        ),
        in_specs=[pl.BlockSpec(memory_space=pltpu.VMEM)] * 2,
        out_specs=[pl.BlockSpec(memory_space=pltpu.HBM)] * 2,
        scratch_shapes=[
            pltpu.VMEM((8, 64, SIDE), F32),
            pltpu.VMEM(tile_shape, BF),
            pltpu.SemaphoreType.DMA((2,)),
        ],
    )(*[pltpu.with_memory_space_constraint(operand, pltpu.VMEM) for operand in (back_blocks, lags)])
    grad_input = grad_input.transpose(0, 2, 1, 3).reshape(rows, width)
    grad_taps = grad_taps.reshape(SIDE, PENCIL, SIDE).transpose(1, 0, 2)
    return grad_input, grad_taps.reshape(1, PENCIL, SIDE * SIDE)


def solution(mesh):
    in_specs = (P(("dp", "chan"), "ctx"), P(("dp", "chan"), "ctx"), P(("dp", "chan"), "ctx", None))
    out_specs = (P(("dp", "chan"), "ctx"), P(("dp", "chan"), "ctx", None))
    return jax.shard_map(shards, mesh=mesh, in_specs=in_specs, out_specs=out_specs, check_vma=False)
```

```python
import math

import jax
import jax.numpy as jnp
import numpy as np
from jax import lax
from jax.experimental import pallas as pl
from jax.experimental.pallas import tpu as pltpu
from jax.sharding import PartitionSpec as P

import ml_dtypes

BF = jnp.bfloat16
F32 = jnp.float32
SIDE = 128
PEERS = 16
BLOCKS = 8
PENCIL = 4
MESH = pl.DeviceIdType.MESH
FAR_FIRST = (
    (3, 2), (3, 1), (3, 3), (2, 2), (2, 1), (2, 3), (3, 0), (1, 2),
    (2, 0), (1, 1), (1, 3), (0, 2), (1, 0), (0, 1), (0, 3),
)


def split_table(values):
    high = values.astype(ml_dtypes.bfloat16)
    low = (values - high.astype(np.float64)).astype(ml_dtypes.bfloat16)
    return high, low


def make_tables():
    total = SIDE * SIDE
    index = np.arange(SIDE, dtype=np.int64)
    first = ((4 * index[:, None] + 1) * index[None, :]) % (4 * SIDE) * (2.0 * np.pi / (4 * SIDE))
    first_high, first_low = split_table(np.concatenate([np.cos(first), -np.sin(first)], axis=0))
    forward_first = np.concatenate([first_high, first_low, first_high], axis=1)
    turn = ((4 * index[:, None] + 1) * index[None, :]) % (4 * total) * (2.0 * np.pi / (4 * total))
    turns = np.stack([np.cos(turn), np.sin(turn)]).astype(np.float32)
    second = (index[:, None] * index[None, :]) % SIDE * (2.0 * np.pi / SIDE)
    cos_two, sin_two = np.cos(second), np.sin(second)
    high, low = split_table(np.block([[cos_two, -sin_two], [sin_two, cos_two]]))
    forward_second = np.concatenate([high, high, low], axis=0)
    high, low = split_table(np.block([[cos_two, sin_two], [-sin_two, cos_two]]))
    inverse_second = np.concatenate([high, high, low], axis=0)
    high, low = split_table(np.concatenate([np.cos(first).T, -np.sin(first).T], axis=1) / total)
    inverse_first = np.concatenate([high, high, low], axis=1)
    short, each = index[:BLOCKS], np.eye(SIDE // BLOCKS)
    first = ((4 * short[:, None] + 1) * short[None, :]) % (4 * BLOCKS) * (2.0 * np.pi / (4 * BLOCKS))
    real, imag = np.kron(each, np.cos(first)), np.kron(each, -np.sin(first))
    high, low = split_table(np.concatenate([real, imag], axis=0))
    local_first = np.concatenate([high, low, high], axis=1)
    high, low = split_table(np.concatenate([real.T, imag.T], axis=1) / (BLOCKS * SIDE))
    local_inverse_first = np.concatenate([high, high, low], axis=1)
    turn = (4 * short[:, None] + 1) * index[None, :] * (2.0 * np.pi / (4 * BLOCKS * SIDE))
    turn = np.tile(turn, (SIDE // BLOCKS, 1))
    local_turns = np.stack([np.cos(turn), np.sin(turn)]).astype(np.float32)
    return (
        forward_first,
        turns,
        forward_second,
        inverse_second,
        inverse_first,
        local_first,
        local_turns,
        local_inverse_first,
    )


def halves(value):
    high = value.astype(BF)
    return high, (value - high.astype(F32)).astype(BF)


def stacked_rows(pairs, turned):
    blocks = []
    for real, imag in pairs:
        real_high, real_low = halves(real)
        imag_high, imag_low = halves(imag)
        parts = [real_high, imag_high, real_low, imag_low, real_high, imag_high]
        blocks.append(jnp.concatenate(parts, axis=0 if turned else 1))
    return jnp.concatenate(blocks, axis=1 if turned else 0)


def channel_parts(spectra):
    count = spectra.shape[0] // SIDE
    return [
        (spectra[at * SIDE : (at + 1) * SIDE, :SIDE], spectra[at * SIDE : (at + 1) * SIDE, SIDE:])
        for at in range(count)
    ]


def second_stage(first, turns_v, second_v):
    cos_turn, sin_turn = turns_v[0], turns_v[1]
    pairs = []
    for at in range(first.shape[1] // SIDE):
        real = first[:SIDE, at * SIDE : (at + 1) * SIDE]
        imag = first[SIDE:, at * SIDE : (at + 1) * SIDE]
        pairs.append((real * cos_turn + imag * sin_turn, imag * cos_turn - real * sin_turn))
    return jnp.dot(stacked_rows(pairs, False), second_v[...], preferred_element_type=F32)


def inverse(pairs, turns_v, inverse_second_v, inverse_first_v):
    mixed = jnp.dot(stacked_rows(pairs, False), inverse_second_v[...], preferred_element_type=F32)
    cos_turn, sin_turn = turns_v[0], turns_v[1]
    turned = [
        (real * cos_turn - imag * sin_turn, imag * cos_turn + real * sin_turn)
        for real, imag in channel_parts(mixed)
    ]
    return jnp.dot(inverse_first_v[...], stacked_rows(turned, True), preferred_element_type=F32)


def forward_wide(blocks, first_v, turns_v, second_v):
    columns = []
    for block in blocks:
        high, low = halves(block)
        columns.append(jnp.concatenate([high, high, low], axis=0))
    first = jnp.dot(first_v[...], jnp.concatenate(columns, axis=1), preferred_element_type=F32)
    return second_stage(first, turns_v, second_v)


def forward(blocks, first_v, turns_v, second_v):
    rows = jnp.concatenate(blocks, axis=1)
    first = jnp.dot(
        first_v[:, : 2 * SIDE], jnp.concatenate([rows, rows], axis=0), preferred_element_type=F32
    )
    return second_stage(first, turns_v, second_v)


def correlation(taken, turned):
    return [
        (turned_real * real + turned_imag * imag, turned_real * imag - turned_imag * real)
        for (real, imag), (turned_real, turned_imag) in zip(channel_parts(taken), channel_parts(turned))
    ]


def kernel(
    grad_hbm,
    input_hbm,
    taps_hbm,
    first_hbm,
    turns_hbm,
    second_hbm,
    inverse_second_hbm,
    inverse_first_hbm,
    local_first_hbm,
    local_turns_hbm,
    local_inverse_first_hbm,
    got_back,
    grad_taps_v,
    grad_v,
    input_v,
    taps_v,
    first_v,
    turns_v,
    second_v,
    inverse_second_v,
    inverse_first_v,
    local_first_v,
    local_turns_v,
    local_inverse_first_v,
    turned_v,
    send_grad,
    send_input,
    send_back,
    got_grad,
    got_input,
    last_grad,
    last_input,
    pass_grad,
    pass_input,
    send_taps,
    send_part,
    got_taps,
    got_part,
    taps_spec,
    grad_spec,
    local_sem,
    send_sem,
    recv_sem,
    entered_sem,
):
    part, me, half = lax.axis_index("dp"), lax.axis_index("ctx"), lax.axis_index("chan")
    in_group = (part == 0) & (half == 0)
    is_last = in_group & (me == 0)
    is_ahead = in_group & (me > 0)
    is_pass = (part == 1) & (half == 0) & (me == 0)
    last_id, pass_id = {"dp": 0, "ctx": 0}, {"dp": 1, "ctx": 0}
    row, column = me // 4, me % 4
    rows = (row, row + 1 - 2 * (row % 2), (row + 2) % 4, 3 - row)
    peers = [rows[over] * 4 + (column + along) % 4 for over, along in FAR_FIRST]

    def load(source, target, slot):
        copy = pltpu.make_async_copy(source, target, local_sem.at[slot])
        copy.start()
        return copy

    grad_load = load(grad_hbm, grad_v, 0)
    input_load = load(input_hbm, input_v, 1)
    taps_load = load(taps_hbm, taps_v, 2)
    table_loads = [
        load(source, target, slot)
        for slot, (source, target) in enumerate(
            (
                (first_hbm, first_v),
                (turns_hbm, turns_v),
                (second_hbm, second_v),
                (inverse_second_hbm, inverse_second_v),
                (inverse_first_hbm, inverse_first_v),
                (local_first_hbm, local_first_v),
                (local_turns_hbm, local_turns_v),
                (local_inverse_first_hbm, local_inverse_first_v),
            ),
            3,
        )
    ]

    barrier = pltpu.get_barrier_semaphore()

    @pl.when(jnp.logical_not(is_last))
    def _():
        for peer in peers:
            pl.semaphore_signal(barrier, inc=1, device_id={"ctx": peer}, device_id_type=MESH)

    @pl.when(is_pass)
    def _():
        for peer in range(PEERS):
            pl.semaphore_signal(barrier, inc=1, device_id={"dp": 0, "ctx": peer}, device_id_type=MESH)

    def turn_rows(source, target):
        for group in range(8):
            turned_v[group] = source[group].astype(F32).reshape(64, SIDE)
            for at in range(8):
                picked = turned_v[group, pl.ds(at, 8, stride=8), :]
                target[2 * group + at // 4, at % 4] = picked.astype(BF)

    def send(source, target, sent, received, device):
        return pltpu.make_async_remote_copy(
            src_ref=source,
            dst_ref=target,
            send_sem=send_sem.at[sent],
            recv_sem=recv_sem.at[received],
            device_id=device,
            device_id_type=MESH,
        )

    def exchange(source, target, slot):
        for peer in peers:

            @pl.when(jnp.logical_not(is_ahead & (peer == 0)))
            def _():
                send(source.at[peer], target.at[me], slot, slot, {"ctx": peer}).start()

        target[me] = source[me]

    def gather(source, target, slot, last, passed):
        @pl.when(is_last)
        def _():
            for peer in peers:
                send(source.at[peer], last, slot, slot + 3, {"ctx": peer}).start()

            target[me] = source[me]

        @pl.when(jnp.logical_not(is_last))
        def _():
            exchange(source, target, slot)

        @pl.when(is_ahead)
        def _():
            send(source.at[0], passed.at[me], slot + 3, slot + 5, pass_id).start()

    def some_of(source, target, count, sent, received):
        return send(
            source.at[pl.ds(0, count)],
            target.at[pl.ds(0, count)],
            sent,
            received,
            {"ctx": peers[0]},
        )

    def all_received(source, target, slot):
        @pl.when(is_ahead)
        def _():
            some_of(source, target, PEERS - 2, slot, slot).wait_recv()

        @pl.when(jnp.logical_not(is_ahead))
        def _():
            some_of(source, target, PEERS - 1, slot, slot).wait_recv()

    grad_load.wait()
    turn_rows(grad_v, send_grad)

    @pl.when(jnp.logical_not(is_last))
    def _():
        pl.semaphore_wait(barrier, PEERS - 1)

    @pl.when(is_last)
    def _():
        pl.semaphore_wait(barrier, PEERS)
        pl.semaphore_signal(entered_sem, inc=1, device_id=pass_id, device_id_type=MESH)

    gather(send_grad, got_grad, 0, last_grad, pass_grad)
    input_load.wait()
    turn_rows(input_v, send_input)
    gather(send_input, got_input, 1, last_input, pass_input)

    taps_load.wait()
    for channel in range(PENCIL):
        send_taps[channel] = taps_v[pl.ds(channel, BLOCKS, stride=PENCIL), :]

    for copy in table_loads:
        copy.wait()

    taps_spec[...] = forward_wide(
        [taps_v[pl.ds(channel, SIDE, stride=PENCIL), :] for channel in range(PENCIL)],
        first_v,
        turns_v,
        second_v,
    )

    def channels(source):
        return [source[:, channel].reshape(SIDE, SIDE) for channel in range(PENCIL)]

    all_received(send_grad, got_grad, 0)

    @pl.when(is_ahead)
    def _():
        got_grad[0] = jnp.zeros_like(got_grad[0])

    grad_spec[...] = forward(channels(got_grad), first_v, turns_v, second_v)
    back = inverse(
        correlation(grad_spec[...], taps_spec[...]), turns_v, inverse_second_v, inverse_first_v
    )
    for channel in range(PENCIL):
        block = back[:, channel * SIDE : (channel + 1) * SIDE]
        send_part[channel] = block[:BLOCKS]
        send_back[:, channel] = block.astype(BF).reshape(PEERS, BLOCKS, SIDE)
    exchange(send_back, got_back, 2)

    all_received(send_input, got_input, 1)

    @pl.when(is_ahead)
    def _():
        send(send_grad.at[0], last_grad, 0, 3, last_id).wait_recv()
        send(send_input.at[0], last_input, 1, 4, last_id).wait_recv()
        send(send_taps, got_taps.at[me], 5, 7, last_id).start()
        send(send_part, got_part.at[me], 6, 8, last_id).start()
        got_grad[0] = last_grad[...]
        got_input[0] = last_input[...]
        grad_spec[...] = forward(channels(got_grad), first_v, turns_v, second_v)

    input_spec = forward(channels(got_input), first_v, turns_v, second_v)
    lags = inverse(
        correlation(grad_spec[...], input_spec), turns_v, inverse_second_v, inverse_first_v
    ) * (1.0 / SIDE)
    for channel in range(PENCIL):
        grad_taps_v[pl.ds(channel, SIDE, stride=PENCIL), :] = lags[:, channel * SIDE : (channel + 1) * SIDE]

    def others(ref):
        return ref.at[pl.ds(1, PEERS - 1)]

    passes = (
        (pass_grad, got_grad, 7, 5, 0),
        (pass_input, got_input, 8, 6, 1),
    )

    @pl.when(is_pass)
    def _():
        for at, (passed, target, sent, arrived, received) in enumerate(passes):
            send(others(passed), others(passed), sent, arrived, last_id).wait_recv()
            if at == 0:
                pl.semaphore_wait(entered_sem, 1)
            send(others(passed), others(target), sent, received, last_id).start()

    @pl.when(is_last)
    def _():
        some_of(got_taps, got_taps, PEERS - 1, 5, 7).wait_recv()
        got_taps[0] = send_taps[...]

        def local_blocks(ref):
            return [ref[at : at + 4].reshape(SIDE, SIDE) for at in range(0, PEERS, 4)]

        local_taps = forward_wide(local_blocks(got_taps), local_first_v, local_turns_v, second_v)
        local_grad = forward(local_blocks(send_grad), local_first_v, local_turns_v, second_v)
        local = inverse(
            correlation(local_grad, local_taps), local_turns_v, inverse_second_v, local_inverse_first_v
        )
        some_of(got_part, got_part, PEERS - 1, 6, 8).wait_recv()
        for at in range(1, PEERS):
            block = local[:, at // 4 * SIDE : (at // 4 + 1) * SIDE].reshape(4, PENCIL, BLOCKS, SIDE)
            got_back[at] = (got_part[at] + block[at % 4]).astype(BF)

    @pl.when(jnp.logical_not(is_last))
    def _():
        some_of(send_back, got_back, PEERS - 1, 2, 2).wait_recv()

    for slot, (source, target) in enumerate(
        ((send_grad, got_grad), (send_input, got_input), (send_back, got_back))
    ):

        @pl.when(is_ahead)
        def _():
            some_of(source, target, PEERS - 2, slot, slot).wait_send()

        @pl.when(jnp.logical_not(is_ahead))
        def _():
            some_of(source, target, PEERS - 1, slot, slot).wait_send()

    @pl.when(is_ahead)
    def _():
        send(send_grad.at[0], last_grad, 3, 5, pass_id).wait_send()
        send(send_input.at[0], last_input, 4, 6, pass_id).wait_send()
        send(send_taps, got_taps.at[me], 5, 7, last_id).wait_send()
        send(send_part, got_part.at[me], 6, 8, last_id).wait_send()

    @pl.when(is_pass)
    def _():
        for passed, target, sent, _, received in passes:
            send(others(passed), others(target), sent, received, last_id).wait_send()


def finish(got_back, grad_taps_v, grad_input_hbm, grad_taps_hbm, turned_v, grad_input_v, sem):
    taps_store = pltpu.make_async_copy(grad_taps_v, grad_taps_hbm, sem.at[0])
    taps_store.start()
    for group in range(8):
        for row in range(8):
            turned_v[group, pl.ds(8 * row, 8), :] = got_back[2 * group + row // 4, row % 4].astype(F32)
        for block in range(8):
            grad_input_v[group, block] = turned_v[group, pl.ds(block, 8, stride=8), :].astype(BF)
    back_store = pltpu.make_async_copy(grad_input_v, grad_input_hbm, sem.at[1])
    back_store.start()
    taps_store.wait()
    back_store.wait()


def shards(layer_input, grad_output, filter_taps):
    rows, width = layer_input.shape
    blocks = width // SIDE
    tiles = (rows // 8, 8, blocks, SIDE)
    tables = make_tables()
    taps = filter_taps.reshape(PENCIL, SIDE, SIDE).transpose(1, 0, 2).reshape(PENCIL * SIDE, SIDE)
    tile_shape = (rows // 8, blocks, 8, SIDE)
    block_shape = (PEERS, PENCIL, blocks, SIDE)
    operands = (
        grad_output.reshape(tiles).transpose(0, 2, 1, 3),
        layer_input.reshape(tiles).transpose(0, 2, 1, 3),
        taps,
        *[jnp.asarray(table) for table in tables],
    )
    back_blocks, lags = pl.pallas_call(
        kernel,
        name="conv_backward",
        out_shape=(
            pltpu.VMEM(block_shape, BF),
            pltpu.VMEM((PENCIL * SIDE, SIDE), F32),
        ),
        in_specs=[pl.BlockSpec(memory_space=pltpu.HBM)] * len(operands),
        out_specs=[pl.BlockSpec(memory_space=pltpu.VMEM)] * 2,
        scratch_shapes=[
            pltpu.VMEM(tile_shape, BF),
            pltpu.VMEM(tile_shape, BF),
            pltpu.VMEM((PENCIL * SIDE, SIDE), F32),
            *[pltpu.VMEM(table.shape, F32 if table.dtype == np.float32 else BF) for table in tables],
            pltpu.VMEM((8, 64, SIDE), F32),
            *[pltpu.VMEM(block_shape, BF)] * 5,
            *[pltpu.VMEM(block_shape[1:], BF)] * 2,
            *[pltpu.VMEM(block_shape, BF)] * 2,
            *[pltpu.VMEM(block_shape[1:], F32)] * 2,
            *[pltpu.VMEM(block_shape, F32)] * 2,
            *[pltpu.VMEM((PENCIL * SIDE, 2 * SIDE), F32)] * 2,
            pltpu.SemaphoreType.DMA((11,)),
            pltpu.SemaphoreType.DMA((9,)),
            pltpu.SemaphoreType.DMA((9,)),
            pltpu.SemaphoreType.REGULAR,
        ],
        compiler_params=pltpu.CompilerParams(
            collective_id=0, has_side_effects=True, vmem_limit_bytes=48 * 1024 * 1024
        ),
    )(*[pltpu.with_memory_space_constraint(operand, pltpu.HBM) for operand in operands])
    grad_input, grad_taps = pl.pallas_call(
        finish,
        name="conv_backward_finish",
        out_shape=(
            jax.ShapeDtypeStruct(tile_shape, BF),
            jax.ShapeDtypeStruct((PENCIL * SIDE, SIDE), F32),
        ),
        in_specs=[pl.BlockSpec(memory_space=pltpu.VMEM)] * 2,
        out_specs=[pl.BlockSpec(memory_space=pltpu.HBM)] * 2,
        scratch_shapes=[
            pltpu.VMEM((8, 64, SIDE), F32),
            pltpu.VMEM(tile_shape, BF),
            pltpu.SemaphoreType.DMA((2,)),
        ],
    )(*[pltpu.with_memory_space_constraint(operand, pltpu.VMEM) for operand in (back_blocks, lags)])
    grad_input = grad_input.transpose(0, 2, 1, 3).reshape(rows, width)
    grad_taps = grad_taps.reshape(SIDE, PENCIL, SIDE).transpose(1, 0, 2)
    return grad_input, grad_taps.reshape(1, PENCIL, SIDE * SIDE)


def solution(mesh):
    in_specs = (P(("dp", "chan"), "ctx"), P(("dp", "chan"), "ctx"), P(("dp", "chan"), "ctx", None))
    out_specs = (P(("dp", "chan"), "ctx"), P(("dp", "chan"), "ctx", None))
    return jax.shard_map(shards, mesh=mesh, in_specs=in_specs, out_specs=out_specs, check_vma=False)
```

```python
import math

import jax
import jax.numpy as jnp
import numpy as np
from jax import lax
from jax.experimental import pallas as pl
from jax.experimental.pallas import tpu as pltpu
from jax.sharding import PartitionSpec as P

import ml_dtypes

BF = jnp.bfloat16
F32 = jnp.float32
SIDE = 128
PEERS = 16
BLOCKS = 8
PENCIL = 4
MESH = pl.DeviceIdType.MESH
FAR_FIRST = (
    (3, 2), (3, 1), (3, 3), (2, 2), (2, 1), (2, 3), (3, 0), (1, 2),
    (2, 0), (1, 1), (1, 3), (0, 2), (1, 0), (0, 1), (0, 3),
)


def split_table(values):
    high = values.astype(ml_dtypes.bfloat16)
    low = (values - high.astype(np.float64)).astype(ml_dtypes.bfloat16)
    return high, low


def make_tables():
    total = SIDE * SIDE
    index = np.arange(SIDE, dtype=np.int64)
    first = ((4 * index[:, None] + 1) * index[None, :]) % (4 * SIDE) * (2.0 * np.pi / (4 * SIDE))
    first_high, first_low = split_table(np.concatenate([np.cos(first), -np.sin(first)], axis=0))
    forward_first = np.concatenate([first_high, first_low, first_high], axis=1)
    turn = ((4 * index[:, None] + 1) * index[None, :]) % (4 * total) * (2.0 * np.pi / (4 * total))
    turns = np.stack([np.cos(turn), np.sin(turn)]).astype(np.float32)
    second = (index[:, None] * index[None, :]) % SIDE * (2.0 * np.pi / SIDE)
    cos_two, sin_two = np.cos(second), np.sin(second)
    high, low = split_table(np.block([[cos_two, -sin_two], [sin_two, cos_two]]))
    forward_second = np.concatenate([high, high, low], axis=0)
    high, low = split_table(np.block([[cos_two, sin_two], [-sin_two, cos_two]]))
    inverse_second = np.concatenate([high, high, low], axis=0)
    high, low = split_table(np.concatenate([np.cos(first).T, -np.sin(first).T], axis=1) / total)
    inverse_first = np.concatenate([high, high, low], axis=1)
    short, each = index[:BLOCKS], np.eye(SIDE // BLOCKS)
    first = ((4 * short[:, None] + 1) * short[None, :]) % (4 * BLOCKS) * (2.0 * np.pi / (4 * BLOCKS))
    real, imag = np.kron(each, np.cos(first)), np.kron(each, -np.sin(first))
    high, low = split_table(np.concatenate([real, imag], axis=0))
    local_first = np.concatenate([high, low, high], axis=1)
    high, low = split_table(np.concatenate([real.T, imag.T], axis=1) / (BLOCKS * SIDE))
    local_inverse_first = np.concatenate([high, high, low], axis=1)
    turn = (4 * short[:, None] + 1) * index[None, :] * (2.0 * np.pi / (4 * BLOCKS * SIDE))
    turn = np.tile(turn, (SIDE // BLOCKS, 1))
    local_turns = np.stack([np.cos(turn), np.sin(turn)]).astype(np.float32)
    return (
        forward_first,
        turns,
        forward_second,
        inverse_second,
        inverse_first,
        local_first,
        local_turns,
        local_inverse_first,
    )


def halves(value):
    high = value.astype(BF)
    return high, (value - high.astype(F32)).astype(BF)


def stacked_rows(pairs, turned):
    blocks = []
    for real, imag in pairs:
        real_high, real_low = halves(real)
        imag_high, imag_low = halves(imag)
        parts = [real_high, imag_high, real_low, imag_low, real_high, imag_high]
        blocks.append(jnp.concatenate(parts, axis=0 if turned else 1))
    return jnp.concatenate(blocks, axis=1 if turned else 0)


def channel_parts(spectra):
    count = spectra.shape[0] // SIDE
    return [
        (spectra[at * SIDE : (at + 1) * SIDE, :SIDE], spectra[at * SIDE : (at + 1) * SIDE, SIDE:])
        for at in range(count)
    ]


def second_stage(first, turns_v, second_v):
    cos_turn, sin_turn = turns_v[0], turns_v[1]
    pairs = []
    for at in range(first.shape[1] // SIDE):
        real = first[:SIDE, at * SIDE : (at + 1) * SIDE]
        imag = first[SIDE:, at * SIDE : (at + 1) * SIDE]
        pairs.append((real * cos_turn + imag * sin_turn, imag * cos_turn - real * sin_turn))
    return jnp.dot(stacked_rows(pairs, False), second_v[...], preferred_element_type=F32)


def inverse(pairs, turns_v, inverse_second_v, inverse_first_v):
    mixed = jnp.dot(stacked_rows(pairs, False), inverse_second_v[...], preferred_element_type=F32)
    cos_turn, sin_turn = turns_v[0], turns_v[1]
    turned = [
        (real * cos_turn - imag * sin_turn, imag * cos_turn + real * sin_turn)
        for real, imag in channel_parts(mixed)
    ]
    return jnp.dot(inverse_first_v[...], stacked_rows(turned, True), preferred_element_type=F32)


def forward_wide(blocks, first_v, turns_v, second_v):
    columns = []
    for block in blocks:
        high, low = halves(block)
        columns.append(jnp.concatenate([high, high, low], axis=0))
    first = jnp.dot(first_v[...], jnp.concatenate(columns, axis=1), preferred_element_type=F32)
    return second_stage(first, turns_v, second_v)


def forward(blocks, first_v, turns_v, second_v):
    rows = jnp.concatenate(blocks, axis=1)
    first = jnp.dot(
        first_v[:, : 2 * SIDE], jnp.concatenate([rows, rows], axis=0), preferred_element_type=F32
    )
    return second_stage(first, turns_v, second_v)


def correlation(taken, turned):
    return [
        (turned_real * real + turned_imag * imag, turned_real * imag - turned_imag * real)
        for (real, imag), (turned_real, turned_imag) in zip(channel_parts(taken), channel_parts(turned))
    ]


def kernel(
    grad_hbm,
    input_hbm,
    taps_hbm,
    first_hbm,
    turns_hbm,
    second_hbm,
    inverse_second_hbm,
    inverse_first_hbm,
    local_first_hbm,
    local_turns_hbm,
    local_inverse_first_hbm,
    got_back,
    grad_taps_v,
    grad_v,
    input_v,
    taps_v,
    first_v,
    turns_v,
    second_v,
    inverse_second_v,
    inverse_first_v,
    local_first_v,
    local_turns_v,
    local_inverse_first_v,
    turned_v,
    send_grad,
    send_input,
    send_back,
    got_grad,
    got_input,
    last_grad,
    last_input,
    pass_grad,
    pass_input,
    send_taps,
    send_part,
    got_taps,
    got_part,
    taps_spec,
    grad_spec,
    local_sem,
    send_sem,
    recv_sem,
    entered_sem,
):
    part, me, half = lax.axis_index("dp"), lax.axis_index("ctx"), lax.axis_index("chan")
    in_group = (part == 0) & (half == 0)
    is_last = in_group & (me == 0)
    is_ahead = in_group & (me > 0)
    is_pass = (part == 1) & (half == 0) & (me == 0)
    last_id, pass_id = {"dp": 0, "ctx": 0}, {"dp": 1, "ctx": 0}
    row, column = me // 4, me % 4
    rows = (row, row + 1 - 2 * (row % 2), (row + 2) % 4, 3 - row)
    peers = [rows[over] * 4 + (column + along) % 4 for over, along in FAR_FIRST]

    barrier = pltpu.get_barrier_semaphore()

    @pl.when(jnp.logical_not(is_last))
    def _():
        for peer in peers:
            pl.semaphore_signal(barrier, inc=1, device_id={"ctx": peer}, device_id_type=MESH)

    @pl.when(is_pass)
    def _():
        for peer in range(PEERS):
            pl.semaphore_signal(barrier, inc=1, device_id={"dp": 0, "ctx": peer}, device_id_type=MESH)

    def load(source, target, slot):
        copy = pltpu.make_async_copy(source, target, local_sem.at[slot])
        copy.start()
        return copy

    grad_load = load(grad_hbm, grad_v, 0)
    input_load = load(input_hbm, input_v, 1)
    taps_load = load(taps_hbm, taps_v, 2)
    table_loads = [
        load(source, target, slot)
        for slot, (source, target) in enumerate(
            (
                (first_hbm, first_v),
                (turns_hbm, turns_v),
                (second_hbm, second_v),
                (inverse_second_hbm, inverse_second_v),
                (inverse_first_hbm, inverse_first_v),
                (local_first_hbm, local_first_v),
                (local_turns_hbm, local_turns_v),
                (local_inverse_first_hbm, local_inverse_first_v),
            ),
            3,
        )
    ]

    def turn_rows(source, target):
        for group in range(8):
            turned_v[group] = source[group].astype(F32).reshape(64, SIDE)
            for at in range(8):
                picked = turned_v[group, pl.ds(at, 8, stride=8), :]
                target[2 * group + at // 4, at % 4] = picked.astype(BF)

    def send(source, target, sent, received, device):
        return pltpu.make_async_remote_copy(
            src_ref=source,
            dst_ref=target,
            send_sem=send_sem.at[sent],
            recv_sem=recv_sem.at[received],
            device_id=device,
            device_id_type=MESH,
        )

    def exchange(source, target, slot):
        for peer in peers:

            @pl.when(jnp.logical_not(is_ahead & (peer == 0)))
            def _():
                send(source.at[peer], target.at[me], slot, slot, {"ctx": peer}).start()

        target[me] = source[me]

    def gather(source, target, slot, last, passed):
        @pl.when(is_last)
        def _():
            for peer in peers:
                send(source.at[peer], last, slot, slot + 3, {"ctx": peer}).start()

            target[me] = source[me]

        @pl.when(jnp.logical_not(is_last))
        def _():
            exchange(source, target, slot)

        @pl.when(is_ahead)
        def _():
            send(source.at[0], passed.at[me], slot + 3, slot + 5, pass_id).start()

    def some_of(source, target, count, sent, received):
        return send(
            source.at[pl.ds(0, count)],
            target.at[pl.ds(0, count)],
            sent,
            received,
            {"ctx": peers[0]},
        )

    def all_received(source, target, slot):
        @pl.when(is_ahead)
        def _():
            some_of(source, target, PEERS - 2, slot, slot).wait_recv()

        @pl.when(jnp.logical_not(is_ahead))
        def _():
            some_of(source, target, PEERS - 1, slot, slot).wait_recv()

    @pl.when(is_last)
    def _():
        pl.semaphore_wait(barrier, PEERS)
        pl.semaphore_signal(entered_sem, inc=1, device_id=pass_id, device_id_type=MESH)

    grad_load.wait()
    turn_rows(grad_v, send_grad)

    @pl.when(jnp.logical_not(is_last))
    def _():
        pl.semaphore_wait(barrier, PEERS - 1)

    gather(send_grad, got_grad, 0, last_grad, pass_grad)
    input_load.wait()
    turn_rows(input_v, send_input)
    gather(send_input, got_input, 1, last_input, pass_input)

    taps_load.wait()
    for channel in range(PENCIL):
        send_taps[channel] = taps_v[pl.ds(channel, BLOCKS, stride=PENCIL), :]

    for copy in table_loads[:3]:
        copy.wait()

    taps_spec[...] = forward_wide(
        [taps_v[pl.ds(channel, SIDE, stride=PENCIL), :] for channel in range(PENCIL)],
        first_v,
        turns_v,
        second_v,
    )

    for copy in table_loads[3:5]:
        copy.wait()

    def channels(source):
        return [source[:, channel].reshape(SIDE, SIDE) for channel in range(PENCIL)]

    all_received(send_grad, got_grad, 0)

    @pl.when(is_ahead)
    def _():
        got_grad[0] = jnp.zeros_like(got_grad[0])

    grad_spec[...] = forward(channels(got_grad), first_v, turns_v, second_v)
    back = inverse(
        correlation(grad_spec[...], taps_spec[...]), turns_v, inverse_second_v, inverse_first_v
    )
    for channel in range(PENCIL):
        block = back[:, channel * SIDE : (channel + 1) * SIDE]
        send_part[channel] = block[:BLOCKS]
        send_back[:, channel] = block.astype(BF).reshape(PEERS, BLOCKS, SIDE)
    exchange(send_back, got_back, 2)

    for copy in table_loads[5:]:
        copy.wait()

    all_received(send_input, got_input, 1)

    @pl.when(is_ahead)
    def _():
        send(send_grad.at[0], last_grad, 0, 3, last_id).wait_recv()
        send(send_taps, got_taps.at[me], 5, 7, last_id).start()
        send(send_part, got_part.at[me], 6, 8, last_id).start()
        got_grad[0] = last_grad[...]
        grad_spec[...] = forward(channels(got_grad), first_v, turns_v, second_v)
        send(send_input.at[0], last_input, 1, 4, last_id).wait_recv()
        got_input[0] = last_input[...]

    input_spec = forward(channels(got_input), first_v, turns_v, second_v)
    lags = inverse(
        correlation(grad_spec[...], input_spec), turns_v, inverse_second_v, inverse_first_v
    ) * (1.0 / SIDE)
    for channel in range(PENCIL):
        grad_taps_v[pl.ds(channel, SIDE, stride=PENCIL), :] = lags[:, channel * SIDE : (channel + 1) * SIDE]

    def others(ref):
        return ref.at[pl.ds(1, PEERS - 1)]

    passes = (
        (pass_grad, got_grad, 7, 5, 0),
        (pass_input, got_input, 8, 6, 1),
    )

    @pl.when(is_pass)
    def _():
        for at, (passed, target, sent, arrived, received) in enumerate(passes):
            send(others(passed), others(passed), sent, arrived, last_id).wait_recv()
            if at == 0:
                pl.semaphore_wait(entered_sem, 1)
            send(others(passed), others(target), sent, received, last_id).start()

    @pl.when(is_last)
    def _():
        some_of(got_taps, got_taps, PEERS - 1, 5, 7).wait_recv()
        got_taps[0] = send_taps[...]

        def local_blocks(ref):
            return [ref[at : at + 4].reshape(SIDE, SIDE) for at in range(0, PEERS, 4)]

        local_taps = forward_wide(local_blocks(got_taps), local_first_v, local_turns_v, second_v)
        local_grad = forward(local_blocks(send_grad), local_first_v, local_turns_v, second_v)
        local = inverse(
            correlation(local_grad, local_taps), local_turns_v, inverse_second_v, local_inverse_first_v
        )
        some_of(got_part, got_part, PEERS - 1, 6, 8).wait_recv()
        for at in range(1, PEERS):
            block = local[:, at // 4 * SIDE : (at // 4 + 1) * SIDE].reshape(4, PENCIL, BLOCKS, SIDE)
            got_back[at] = (got_part[at] + block[at % 4]).astype(BF)

    @pl.when(jnp.logical_not(is_last))
    def _():
        some_of(send_back, got_back, PEERS - 1, 2, 2).wait_recv()

    for slot, (source, target) in enumerate(
        ((send_grad, got_grad), (send_input, got_input), (send_back, got_back))
    ):

        @pl.when(is_ahead)
        def _():
            some_of(source, target, PEERS - 2, slot, slot).wait_send()

        @pl.when(jnp.logical_not(is_ahead))
        def _():
            some_of(source, target, PEERS - 1, slot, slot).wait_send()

    @pl.when(is_ahead)
    def _():
        send(send_grad.at[0], last_grad, 3, 5, pass_id).wait_send()
        send(send_input.at[0], last_input, 4, 6, pass_id).wait_send()
        send(send_taps, got_taps.at[me], 5, 7, last_id).wait_send()
        send(send_part, got_part.at[me], 6, 8, last_id).wait_send()

    @pl.when(is_pass)
    def _():
        for passed, target, sent, _, received in passes:
            send(others(passed), others(target), sent, received, last_id).wait_send()


def finish(got_back, grad_taps_v, grad_input_hbm, grad_taps_hbm, turned_v, grad_input_v, sem):
    taps_store = pltpu.make_async_copy(grad_taps_v, grad_taps_hbm, sem.at[0])
    taps_store.start()
    for group in range(8):
        for row in range(8):
            turned_v[group, pl.ds(8 * row, 8), :] = got_back[2 * group + row // 4, row % 4].astype(F32)
        for block in range(8):
            grad_input_v[group, block] = turned_v[group, pl.ds(block, 8, stride=8), :].astype(BF)
    back_store = pltpu.make_async_copy(grad_input_v, grad_input_hbm, sem.at[1])
    back_store.start()
    taps_store.wait()
    back_store.wait()


def shards(layer_input, grad_output, filter_taps):
    rows, width = layer_input.shape
    blocks = width // SIDE
    tiles = (rows // 8, 8, blocks, SIDE)
    tables = make_tables()
    taps = filter_taps.reshape(PENCIL, SIDE, SIDE).transpose(1, 0, 2).reshape(PENCIL * SIDE, SIDE)
    tile_shape = (rows // 8, blocks, 8, SIDE)
    block_shape = (PEERS, PENCIL, blocks, SIDE)
    operands = (
        grad_output.reshape(tiles).transpose(0, 2, 1, 3),
        layer_input.reshape(tiles).transpose(0, 2, 1, 3),
        taps,
        *[jnp.asarray(table) for table in tables],
    )
    back_blocks, lags = pl.pallas_call(
        kernel,
        name="conv_backward",
        out_shape=(
            pltpu.VMEM(block_shape, BF),
            pltpu.VMEM((PENCIL * SIDE, SIDE), F32),
        ),
        in_specs=[pl.BlockSpec(memory_space=pltpu.HBM)] * len(operands),
        out_specs=[pl.BlockSpec(memory_space=pltpu.VMEM)] * 2,
        scratch_shapes=[
            pltpu.VMEM(tile_shape, BF),
            pltpu.VMEM(tile_shape, BF),
            pltpu.VMEM((PENCIL * SIDE, SIDE), F32),
            *[pltpu.VMEM(table.shape, F32 if table.dtype == np.float32 else BF) for table in tables],
            pltpu.VMEM((8, 64, SIDE), F32),
            *[pltpu.VMEM(block_shape, BF)] * 5,
            *[pltpu.VMEM(block_shape[1:], BF)] * 2,
            *[pltpu.VMEM(block_shape, BF)] * 2,
            *[pltpu.VMEM(block_shape[1:], F32)] * 2,
            *[pltpu.VMEM(block_shape, F32)] * 2,
            *[pltpu.VMEM((PENCIL * SIDE, 2 * SIDE), F32)] * 2,
            pltpu.SemaphoreType.DMA((11,)),
            pltpu.SemaphoreType.DMA((9,)),
            pltpu.SemaphoreType.DMA((9,)),
            pltpu.SemaphoreType.REGULAR,
        ],
        compiler_params=pltpu.CompilerParams(
            collective_id=0, has_side_effects=True, vmem_limit_bytes=48 * 1024 * 1024
        ),
    )(*[pltpu.with_memory_space_constraint(operand, pltpu.HBM) for operand in operands])
    grad_input, grad_taps = pl.pallas_call(
        finish,
        name="conv_backward_finish",
        out_shape=(
            jax.ShapeDtypeStruct(tile_shape, BF),
            jax.ShapeDtypeStruct((PENCIL * SIDE, SIDE), F32),
        ),
        in_specs=[pl.BlockSpec(memory_space=pltpu.VMEM)] * 2,
        out_specs=[pl.BlockSpec(memory_space=pltpu.HBM)] * 2,
        scratch_shapes=[
            pltpu.VMEM((8, 64, SIDE), F32),
            pltpu.VMEM(tile_shape, BF),
            pltpu.SemaphoreType.DMA((2,)),
        ],
    )(*[pltpu.with_memory_space_constraint(operand, pltpu.VMEM) for operand in (back_blocks, lags)])
    grad_input = grad_input.transpose(0, 2, 1, 3).reshape(rows, width)
    grad_taps = grad_taps.reshape(SIDE, PENCIL, SIDE).transpose(1, 0, 2)
    return grad_input, grad_taps.reshape(1, PENCIL, SIDE * SIDE)


def solution(mesh):
    in_specs = (P(("dp", "chan"), "ctx"), P(("dp", "chan"), "ctx"), P(("dp", "chan"), "ctx", None))
    out_specs = (P(("dp", "chan"), "ctx"), P(("dp", "chan"), "ctx", None))
    return jax.shard_map(shards, mesh=mesh, in_specs=in_specs, out_specs=out_specs, check_vma=False)
```

```python
import math

import jax
import jax.numpy as jnp
import numpy as np
from jax import lax
from jax.experimental import pallas as pl
from jax.experimental.pallas import tpu as pltpu
from jax.sharding import PartitionSpec as P

import ml_dtypes

BF = jnp.bfloat16
F32 = jnp.float32
SIDE = 128
PEERS = 16
BLOCKS = 8
PENCIL = 4
MESH = pl.DeviceIdType.MESH
FAR_FIRST = (
    (3, 2), (3, 1), (3, 3), (2, 2), (2, 1), (2, 3), (3, 0), (1, 2),
    (2, 0), (1, 1), (1, 3), (0, 2), (1, 0), (0, 1), (0, 3),
)


def wide_rows(table_v):
    half = table_v.shape[0] // 2
    return jnp.concatenate([table_v[:half], table_v[:half], table_v[half:]], axis=0)


def wide_columns(table_v):
    half = table_v.shape[0] // 2
    return jnp.concatenate([table_v[:half], table_v[:half], table_v[half:]], axis=1)


def split_table(values):
    high = values.astype(ml_dtypes.bfloat16)
    low = (values - high.astype(np.float64)).astype(ml_dtypes.bfloat16)
    return high, low


def make_tables():
    total = SIDE * SIDE
    index = np.arange(SIDE, dtype=np.int64)
    first = ((4 * index[:, None] + 1) * index[None, :]) % (4 * SIDE) * (2.0 * np.pi / (4 * SIDE))
    first_high, first_low = split_table(np.concatenate([np.cos(first), -np.sin(first)], axis=0))
    forward_first = np.concatenate([first_high, first_low], axis=1)
    turn = ((4 * index[:, None] + 1) * index[None, :]) % (4 * total) * (2.0 * np.pi / (4 * total))
    turns = np.stack([np.cos(turn), np.sin(turn)]).astype(np.float32)
    second = (index[:, None] * index[None, :]) % SIDE * (2.0 * np.pi / SIDE)
    cos_two, sin_two = np.cos(second), np.sin(second)
    high, low = split_table(np.block([[cos_two, -sin_two], [sin_two, cos_two]]))
    forward_second = np.concatenate([high, low], axis=0)
    high, low = split_table(np.block([[cos_two, sin_two], [-sin_two, cos_two]]))
    inverse_second = np.concatenate([high, low], axis=0)
    high, low = split_table(np.concatenate([np.cos(first).T, -np.sin(first).T], axis=1) / total)
    inverse_first = np.concatenate([high, low], axis=0)
    short, each = index[:BLOCKS], np.eye(SIDE // BLOCKS)
    first = ((4 * short[:, None] + 1) * short[None, :]) % (4 * BLOCKS) * (2.0 * np.pi / (4 * BLOCKS))
    real, imag = np.kron(each, np.cos(first)), np.kron(each, -np.sin(first))
    high, low = split_table(np.concatenate([real, imag], axis=0))
    local_first = np.concatenate([high, low], axis=1)
    high, low = split_table(np.concatenate([real.T, imag.T], axis=1) / (BLOCKS * SIDE))
    local_inverse_first = np.concatenate([high, low], axis=0)
    turn = (4 * short[:, None] + 1) * index[None, :] * (2.0 * np.pi / (4 * BLOCKS * SIDE))
    turn = np.tile(turn, (SIDE // BLOCKS, 1))
    local_turns = np.stack([np.cos(turn), np.sin(turn)]).astype(np.float32)
    parts = (forward_first, forward_second, inverse_second, inverse_first, local_first, local_inverse_first)
    return np.concatenate(parts, axis=0), np.concatenate([turns, local_turns], axis=0)


def table_views(tables_v, turns_v):
    views, start = [], 0
    for count in (2 * SIDE, 4 * SIDE, 4 * SIDE, 2 * SIDE, 2 * SIDE, 2 * SIDE):
        views.append(tables_v.at[start : start + count])
        start += count
    return views, turns_v.at[:2], turns_v.at[2:]


def halves(value):
    high = value.astype(BF)
    return high, (value - high.astype(F32)).astype(BF)


def stacked_rows(pairs, turned):
    blocks = []
    for real, imag in pairs:
        real_high, real_low = halves(real)
        imag_high, imag_low = halves(imag)
        parts = [real_high, imag_high, real_low, imag_low, real_high, imag_high]
        blocks.append(jnp.concatenate(parts, axis=0 if turned else 1))
    return jnp.concatenate(blocks, axis=1 if turned else 0)


def channel_parts(spectra):
    count = spectra.shape[0] // SIDE
    return [
        (spectra[at * SIDE : (at + 1) * SIDE, :SIDE], spectra[at * SIDE : (at + 1) * SIDE, SIDE:])
        for at in range(count)
    ]


def second_stage(first, turns_v, second_v):
    cos_turn, sin_turn = turns_v[0], turns_v[1]
    pairs = []
    for at in range(first.shape[1] // SIDE):
        real = first[:SIDE, at * SIDE : (at + 1) * SIDE]
        imag = first[SIDE:, at * SIDE : (at + 1) * SIDE]
        pairs.append((real * cos_turn + imag * sin_turn, imag * cos_turn - real * sin_turn))
    return jnp.dot(stacked_rows(pairs, False), wide_rows(second_v), preferred_element_type=F32)


def inverse(pairs, turns_v, inverse_second_v, inverse_first_v):
    mixed = jnp.dot(stacked_rows(pairs, False), wide_rows(inverse_second_v), preferred_element_type=F32)
    cos_turn, sin_turn = turns_v[0], turns_v[1]
    turned = [
        (real * cos_turn - imag * sin_turn, imag * cos_turn + real * sin_turn)
        for real, imag in channel_parts(mixed)
    ]
    return jnp.dot(wide_columns(inverse_first_v), stacked_rows(turned, True), preferred_element_type=F32)


def forward_wide(blocks, first_v, turns_v, second_v):
    columns = []
    for block in blocks:
        high, low = halves(block)
        columns.append(jnp.concatenate([high, high, low], axis=0))
    table = jnp.concatenate([first_v[...], first_v[:, :SIDE]], axis=1)
    first = jnp.dot(table, jnp.concatenate(columns, axis=1), preferred_element_type=F32)
    return second_stage(first, turns_v, second_v)


def forward(blocks, first_v, turns_v, second_v):
    rows = jnp.concatenate(blocks, axis=1)
    first = jnp.dot(
        first_v[...], jnp.concatenate([rows, rows], axis=0), preferred_element_type=F32
    )
    return second_stage(first, turns_v, second_v)


def correlation(taken, turned):
    return [
        (turned_real * real + turned_imag * imag, turned_real * imag - turned_imag * real)
        for (real, imag), (turned_real, turned_imag) in zip(channel_parts(taken), channel_parts(turned))
    ]


def kernel(
    grad_hbm,
    input_hbm,
    taps_hbm,
    tables_hbm,
    turns_hbm,
    got_back,
    grad_taps_v,
    grad_v,
    input_v,
    taps_v,
    tables_v,
    all_turns_v,
    turned_v,
    send_grad,
    send_input,
    send_back,
    got_grad,
    got_input,
    last_grad,
    last_input,
    pass_grad,
    pass_input,
    send_taps,
    send_part,
    got_taps,
    got_part,
    taps_spec,
    grad_spec,
    local_sem,
    send_sem,
    recv_sem,
    entered_sem,
):
    part, me, half = lax.axis_index("dp"), lax.axis_index("ctx"), lax.axis_index("chan")
    in_group = (part == 0) & (half == 0)
    is_last = in_group & (me == 0)
    is_ahead = in_group & (me > 0)
    is_pass = (part == 1) & (half == 0) & (me == 0)
    last_id, pass_id = {"dp": 0, "ctx": 0}, {"dp": 1, "ctx": 0}
    row, column = me // 4, me % 4
    rows = (row, row + 1 - 2 * (row % 2), (row + 2) % 4, 3 - row)
    peers = [rows[over] * 4 + (column + along) % 4 for over, along in FAR_FIRST]

    barrier = pltpu.get_barrier_semaphore()

    @pl.when(jnp.logical_not(is_last))
    def _():
        for peer in peers:
            pl.semaphore_signal(barrier, inc=1, device_id={"ctx": peer}, device_id_type=MESH)

    @pl.when(is_pass)
    def _():
        for peer in range(PEERS):
            pl.semaphore_signal(barrier, inc=1, device_id={"dp": 0, "ctx": peer}, device_id_type=MESH)

    def load(source, target, slot):
        copy = pltpu.make_async_copy(source, target, local_sem.at[slot])
        copy.start()
        return copy

    grad_load = load(grad_hbm, grad_v, 0)
    input_load = load(input_hbm, input_v, 1)
    taps_load = load(taps_hbm, taps_v, 2)
    table_loads = [load(tables_hbm, tables_v, 3), load(turns_hbm, all_turns_v, 4)]
    views, turns_v, local_turns_v = table_views(tables_v, all_turns_v)
    first_v, second_v, inverse_second_v, inverse_first_v, local_first_v, local_inverse_first_v = views

    def turn_rows(source, target):
        for group in range(8):
            turned_v[group] = source[group].astype(F32).reshape(64, SIDE)
            for at in range(8):
                picked = turned_v[group, pl.ds(at, 8, stride=8), :]
                target[2 * group + at // 4, at % 4] = picked.astype(BF)

    def send(source, target, sent, received, device):
        return pltpu.make_async_remote_copy(
            src_ref=source,
            dst_ref=target,
            send_sem=send_sem.at[sent],
            recv_sem=recv_sem.at[received],
            device_id=device,
            device_id_type=MESH,
        )

    def exchange(source, target, slot):
        for peer in peers:

            @pl.when(jnp.logical_not(is_ahead & (peer == 0)))
            def _():
                send(source.at[peer], target.at[me], slot, slot, {"ctx": peer}).start()

        target[me] = source[me]

    def gather(source, target, slot, last, passed):
        @pl.when(is_last)
        def _():
            for peer in peers:
                send(source.at[peer], last, slot, slot + 3, {"ctx": peer}).start()

            target[me] = source[me]

        @pl.when(jnp.logical_not(is_last))
        def _():
            exchange(source, target, slot)

        @pl.when(is_ahead)
        def _():
            send(source.at[0], passed.at[me], slot + 3, slot + 5, pass_id).start()

    def some_of(source, target, count, sent, received):
        return send(
            source.at[pl.ds(0, count)],
            target.at[pl.ds(0, count)],
            sent,
            received,
            {"ctx": peers[0]},
        )

    def all_received(source, target, slot):
        @pl.when(is_ahead)
        def _():
            some_of(source, target, PEERS - 2, slot, slot).wait_recv()

        @pl.when(jnp.logical_not(is_ahead))
        def _():
            some_of(source, target, PEERS - 1, slot, slot).wait_recv()

    @pl.when(is_last)
    def _():
        pl.semaphore_wait(barrier, PEERS)
        pl.semaphore_signal(entered_sem, inc=1, device_id=pass_id, device_id_type=MESH)

    grad_load.wait()
    turn_rows(grad_v, send_grad)

    @pl.when(jnp.logical_not(is_last))
    def _():
        pl.semaphore_wait(barrier, PEERS - 1)

    gather(send_grad, got_grad, 0, last_grad, pass_grad)
    input_load.wait()
    turn_rows(input_v, send_input)
    gather(send_input, got_input, 1, last_input, pass_input)

    @pl.when(is_last)
    def _():
        for peer in peers:
            pl.semaphore_signal(entered_sem, inc=1, device_id={"ctx": peer}, device_id_type=MESH)

    taps_load.wait()
    for channel in range(PENCIL):
        send_taps[channel] = taps_v[pl.ds(channel, BLOCKS, stride=PENCIL), :]

    for copy in table_loads:
        copy.wait()

    taps_spec[...] = forward_wide(
        [taps_v[pl.ds(channel, SIDE, stride=PENCIL), :] for channel in range(PENCIL)],
        first_v,
        turns_v,
        second_v,
    )

    def channels(source):
        return [source[:, channel].reshape(SIDE, SIDE) for channel in range(PENCIL)]

    all_received(send_grad, got_grad, 0)

    @pl.when(is_ahead)
    def _():
        got_grad[0] = jnp.zeros_like(got_grad[0])

    grad_spec[...] = forward(channels(got_grad), first_v, turns_v, second_v)
    back = inverse(
        correlation(grad_spec[...], taps_spec[...]), turns_v, inverse_second_v, inverse_first_v
    )
    for channel in range(PENCIL):
        block = back[:, channel * SIDE : (channel + 1) * SIDE]
        send_part[channel] = block[:BLOCKS]
        send_back[:, channel] = block.astype(BF).reshape(PEERS, BLOCKS, SIDE)

    @pl.when(is_last)
    def _():
        for peer in reversed(peers):
            send(send_back.at[peer], got_back.at[me], 2, 2, {"ctx": peer}).start()

        got_back[me] = send_back[me]

    @pl.when(jnp.logical_not(is_last))
    def _():
        exchange(send_back, got_back, 2)


    all_received(send_input, got_input, 1)

    @pl.when(is_ahead)
    def _():
        pl.semaphore_wait(entered_sem, 1)
        send(send_taps, got_taps.at[me], 5, 7, last_id).start()
        send(send_part, got_part.at[me], 6, 8, last_id).start()
        send(send_grad.at[0], last_grad, 0, 3, last_id).wait_recv()
        got_grad[0] = last_grad[...]
        grad_spec[...] = forward(channels(got_grad), first_v, turns_v, second_v)
        send(send_input.at[0], last_input, 1, 4, last_id).wait_recv()
        got_input[0] = last_input[...]

    input_spec = forward(channels(got_input), first_v, turns_v, second_v)
    lags = inverse(
        correlation(grad_spec[...], input_spec), turns_v, inverse_second_v, inverse_first_v
    ) * (1.0 / SIDE)
    for channel in range(PENCIL):
        grad_taps_v[pl.ds(channel, SIDE, stride=PENCIL), :] = lags[:, channel * SIDE : (channel + 1) * SIDE]

    def others(ref):
        return ref.at[pl.ds(1, PEERS - 1)]

    passes = (
        (pass_grad, got_grad, 7, 5, 0),
        (pass_input, got_input, 8, 6, 1),
    )

    @pl.when(is_pass)
    def _():
        for at, (passed, target, sent, arrived, received) in enumerate(passes):
            send(others(passed), others(passed), sent, arrived, last_id).wait_recv()
            if at == 0:
                pl.semaphore_wait(entered_sem, 1)
            send(others(passed), others(target), sent, received, last_id).start()

    @pl.when(is_last)
    def _():
        some_of(got_taps, got_taps, PEERS - 1, 5, 7).wait_recv()
        got_taps[0] = send_taps[...]

        def local_blocks(ref):
            return [ref[at : at + 4].reshape(SIDE, SIDE) for at in range(0, PEERS, 4)]

        local_taps = forward_wide(local_blocks(got_taps), local_first_v, local_turns_v, second_v)
        local_grad = forward(local_blocks(send_grad), local_first_v, local_turns_v, second_v)
        local = inverse(
            correlation(local_grad, local_taps), local_turns_v, inverse_second_v, local_inverse_first_v
        )
        some_of(got_part, got_part, PEERS - 1, 6, 8).wait_recv()
        for at in range(1, PEERS):
            block = local[:, at // 4 * SIDE : (at // 4 + 1) * SIDE].reshape(4, PENCIL, BLOCKS, SIDE)
            got_back[at] = (got_part[at] + block[at % 4]).astype(BF)

    @pl.when(jnp.logical_not(is_last))
    def _():
        some_of(send_back, got_back, PEERS - 1, 2, 2).wait_recv()

    for slot, (source, target) in enumerate(
        ((send_grad, got_grad), (send_input, got_input), (send_back, got_back))
    ):

        @pl.when(is_ahead)
        def _():
            some_of(source, target, PEERS - 2, slot, slot).wait_send()

        @pl.when(jnp.logical_not(is_ahead))
        def _():
            some_of(source, target, PEERS - 1, slot, slot).wait_send()

    @pl.when(is_ahead)
    def _():
        send(send_grad.at[0], last_grad, 3, 5, pass_id).wait_send()
        send(send_input.at[0], last_input, 4, 6, pass_id).wait_send()
        send(send_taps, got_taps.at[me], 5, 7, last_id).wait_send()
        send(send_part, got_part.at[me], 6, 8, last_id).wait_send()

    @pl.when(is_pass)
    def _():
        for passed, target, sent, _, received in passes:
            send(others(passed), others(target), sent, received, last_id).wait_send()


def finish(got_back, grad_taps_v, grad_input_hbm, grad_taps_hbm, turned_v, grad_input_v, sem):
    taps_store = pltpu.make_async_copy(grad_taps_v, grad_taps_hbm, sem.at[0])
    taps_store.start()
    for group in range(8):
        for row in range(8):
            turned_v[group, pl.ds(8 * row, 8), :] = got_back[2 * group + row // 4, row % 4].astype(F32)
        for block in range(8):
            grad_input_v[group, block] = turned_v[group, pl.ds(block, 8, stride=8), :].astype(BF)
    back_store = pltpu.make_async_copy(grad_input_v, grad_input_hbm, sem.at[1])
    back_store.start()
    taps_store.wait()
    back_store.wait()


def shards(layer_input, grad_output, filter_taps):
    rows, width = layer_input.shape
    blocks = width // SIDE
    tiles = (rows // 8, 8, blocks, SIDE)
    tables = make_tables()
    taps = filter_taps.reshape(PENCIL, SIDE, SIDE).transpose(1, 0, 2).reshape(PENCIL * SIDE, SIDE)
    tile_shape = (rows // 8, blocks, 8, SIDE)
    block_shape = (PEERS, PENCIL, blocks, SIDE)
    operands = (
        grad_output.reshape(tiles).transpose(0, 2, 1, 3),
        layer_input.reshape(tiles).transpose(0, 2, 1, 3),
        taps,
        *[jnp.asarray(table) for table in tables],
    )
    back_blocks, lags = pl.pallas_call(
        kernel,
        name="conv_backward",
        out_shape=(
            pltpu.VMEM(block_shape, BF),
            pltpu.VMEM((PENCIL * SIDE, SIDE), F32),
        ),
        in_specs=[pl.BlockSpec(memory_space=pltpu.HBM)] * len(operands),
        out_specs=[pl.BlockSpec(memory_space=pltpu.VMEM)] * 2,
        scratch_shapes=[
            pltpu.VMEM(tile_shape, BF),
            pltpu.VMEM(tile_shape, BF),
            pltpu.VMEM((PENCIL * SIDE, SIDE), F32),
            *[pltpu.VMEM(table.shape, F32 if table.dtype == np.float32 else BF) for table in tables],
            pltpu.VMEM((8, 64, SIDE), F32),
            *[pltpu.VMEM(block_shape, BF)] * 5,
            *[pltpu.VMEM(block_shape[1:], BF)] * 2,
            *[pltpu.VMEM(block_shape, BF)] * 2,
            *[pltpu.VMEM(block_shape[1:], F32)] * 2,
            *[pltpu.VMEM(block_shape, F32)] * 2,
            *[pltpu.VMEM((PENCIL * SIDE, 2 * SIDE), F32)] * 2,
            pltpu.SemaphoreType.DMA((5,)),
            pltpu.SemaphoreType.DMA((9,)),
            pltpu.SemaphoreType.DMA((9,)),
            pltpu.SemaphoreType.REGULAR,
        ],
        compiler_params=pltpu.CompilerParams(
            collective_id=0, has_side_effects=True, vmem_limit_bytes=48 * 1024 * 1024
        ),
    )(*[pltpu.with_memory_space_constraint(operand, pltpu.HBM) for operand in operands])
    grad_input, grad_taps = pl.pallas_call(
        finish,
        name="conv_backward_finish",
        out_shape=(
            jax.ShapeDtypeStruct(tile_shape, BF),
            jax.ShapeDtypeStruct((PENCIL * SIDE, SIDE), F32),
        ),
        in_specs=[pl.BlockSpec(memory_space=pltpu.VMEM)] * 2,
        out_specs=[pl.BlockSpec(memory_space=pltpu.HBM)] * 2,
        scratch_shapes=[
            pltpu.VMEM((8, 64, SIDE), F32),
            pltpu.VMEM(tile_shape, BF),
            pltpu.SemaphoreType.DMA((2,)),
        ],
    )(*[pltpu.with_memory_space_constraint(operand, pltpu.VMEM) for operand in (back_blocks, lags)])
    grad_input = grad_input.transpose(0, 2, 1, 3).reshape(rows, width)
    grad_taps = grad_taps.reshape(SIDE, PENCIL, SIDE).transpose(1, 0, 2)
    return grad_input, grad_taps.reshape(1, PENCIL, SIDE * SIDE)


def solution(mesh):
    in_specs = (P(("dp", "chan"), "ctx"), P(("dp", "chan"), "ctx"), P(("dp", "chan"), "ctx", None))
    out_specs = (P(("dp", "chan"), "ctx"), P(("dp", "chan"), "ctx", None))
    return jax.shard_map(shards, mesh=mesh, in_specs=in_specs, out_specs=out_specs, check_vma=False)
```
